32 devices in a mesh: groups: 2 (over y), ep: 4 (over x, core), tp: 4 (over z).
Axes of the slice: x: 2, y: 2, z: 4, core: 2. Of those that a mesh axis runs over, the one named last changes fastest.
Arguments:
- hidden_states: bfloat16 [256, 7168], P(('groups', 'ep', 'tp')), parts along dimension 0, may hold values from -6 to 6
- norm_gain: float32 [7168], replicated, may hold values from 0.1 to 1.9
- expert_ids: int32 [256, 8], P(('groups', 'ep', 'tp')), parts along dimension 0, may hold values from 0 to 15, all different within a row; in each aligned block of 8 rows (0 to 7, 8 to 15, ...) at most 5 rows name the same one
- gate_weights: float32 [256, 8], P(('groups', 'ep', 'tp')), parts along dimension 0, may hold values from 0.1 to 1
- capacity: int32 [16], replicated, may hold values from 3 to 5
- expert_in: bfloat16 [16, 2048, 2, 7168], P('ep', 'tp'), may hold values from -0.0625 to 0.0625
- expert_out: bfloat16 [16, 2048, 7168], P('ep', 'tp'), may hold values from -0.125 to 0.125
Outputs:
- mixed_out: bfloat16 [256, 7168], P(('groups', 'ep', 'tp')), parts along dimension 0
The draws below stay inside these ranges and needn't reach their ends.
There are 2 independent parts, one for each index of `groups`. The reference program is written for one: setup_inputs(seed, part) draws one part's arguments, and reference() takes and returns one part's arrays. A program takes and returns all parts, laid end to end along the dimension named above; an argument that names none is the same for every part. Nothing has to cross between parts.
Inputs may be any that keep to these rules, and one draw needn't show every extreme that they name: `expert_ids`: each row names 8 different experts; within the rows of one device no expert is named more than 5 times.
All inputs are finite; a program needn't handle non-finite values.
Results may differ from the reference program's by a relative error of at most 0.006.
Values may be sent and summed in bfloat16 or wider, within the bound.
No kernel may reach another device: no remote copies, remote signals or barrier semaphores. Data moves between devices by JAX's collectives and lax.ppermute only.
A program may use at most 320 MiB of HBM per device.

```python
import math
import jax
import jax.numpy as jnp
import numpy as np
from jax import lax

D = 7168
F = 2048
TOPK = 8
EXPERTS = 16
TOK_DEV = 8
CAP = 5
TOKENS = 128
N_EP = 4
N_TP = 4


def touch_ends(result, rng, least, top_value):
    dims = result.shape
    index_at = [jax.random.randint(jax.random.fold_in(rng, axis), (), 0, dims[axis]) for axis in range(len(dims))]
    result = result.at[tuple(index_at)].set(least)
    longest = dims.index(max(dims))
    index_at[longest] = (index_at[longest] + 1) % dims[longest]
    return result.at[tuple(index_at)].set(top_value)


def steps_of(rng, extent, split, least, largest):
    factor_of, own = 1.0, jax.random.fold_in(rng, 6)
    for axis_at, blocks in split:
        draws = jnp.exp(jax.random.uniform(jax.random.fold_in(own, axis_at), (blocks,), jnp.float32, least / len(split), largest / len(split)))
        factor_of = factor_of * jnp.repeat(draws, extent[axis_at] // blocks).reshape([-1 if axis == axis_at else 1 for axis in range(len(extent))])
    return factor_of


def assign_block(stream_key, own, number, rows, number_of, top, reach, slope):
    order = jax.random.permutation(stream_key, number_of)
    packed, ordinary = shares(number_of, rows * top, reach, slope, True), shares(number_of, rows * top, reach, slope, False)
    places = jnp.arange(number_of)

    def named(lengths, offset_by):
        used = int((lengths > 0).sum())
        fixed = max(1, used // 4)
        passed = fixed + (places - fixed + offset_by * (used - fixed)) % max(1, number_of - fixed)
        return jnp.zeros((number_of,), jnp.int32).at[order[jnp.where(places < fixed, places, passed)]].set(jnp.asarray(lengths, jnp.int32))

    lengths = jnp.where(number % 4 == 0, named(packed, number // 4), named(ordinary, number - number // 4 - 1))
    mixed = jax.random.permutation(jax.random.fold_in(own, 3), number_of)
    giver, taker = mixed[0:number_of // 2 * 2:2], mixed[1:number_of // 2 * 2:2]
    margin = jnp.minimum(lengths[giver] - 1, reach - lengths[taker]) // 2
    margin = jnp.where((giver == order[0]) | (taker == order[0]) | (lengths[taker] == 0), 0, jnp.maximum(margin, 0))
    passed = jax.random.randint(jax.random.fold_in(own, 4), (number_of // 2,), 0, 1 << 20) % (margin + 1)
    lengths = lengths.at[giver].add(-passed).at[taker].add(passed)
    members = jnp.searchsorted(jnp.cumsum(lengths), jnp.arange(rows * top), side="right").astype(jnp.int32)
    table = members.reshape(top, rows).T
    table = table[jax.random.permutation(jax.random.fold_in(own, 1), rows)]
    offset_by = jax.random.randint(jax.random.fold_in(own, 2), (rows, 1), 0, top)
    return jnp.take_along_axis(table, (jnp.arange(top)[None, :] + offset_by) % top, axis=1)


def shares(number_of, total, reach, slope, full):
    portions = [(1 << 20) // math.isqrt(rank ** slope) + 1 for rank in range(1, number_of + 1)]
    largest = reach if full else min(reach, max(-(-total // number_of), total * portions[0] // sum(portions)))
    least = 1 if total - largest >= number_of - 1 else 0
    given, surplus = [largest] + [least] * (number_of - 1), total - largest - least * (number_of - 1)
    while surplus > 0:
        candidates = [i for i in range(1, number_of) if given[i] < largest] or [i for i in range(1, number_of) if given[i] < reach]
        pool, budget = sum([portions[i] for i in candidates]), surplus
        for i in candidates:
            extra = min(reach - given[i], max(1, budget * portions[i] // pool), surplus)
            given[i] = given[i] + extra
            surplus = surplus - extra
    return np.array(given)


def scatter_about(key, shape, width, limit, split=(), held_as=jnp.bfloat16):
    loudness = steps_of(key, shape, split, -0.22, 0.18) if split else 1.0
    array = jax.random.normal(key, shape, jnp.float32) * width * loudness
    return jnp.minimum(jnp.maximum(array, -limit), limit).astype(held_as)


def setup_inputs(seed: int = 0, part: int = 0) -> dict:
    arg_keys = jax.random.split(jax.random.key(seed), 8)
    own_keys = jax.random.split(jax.random.fold_in(arg_keys[7], part), 8)
    hidden_states = scatter_about(own_keys[0], (TOKENS, D), 1.0, 6.0, ((0, 16),))
    norm_gain = jnp.clip(1.0 + 0.18 * jax.random.normal(arg_keys[1], (D,), jnp.float32), 0.1, 1.9)
    expert_ids_keys = jax.random.split(jax.random.fold_in(own_keys[2], 1), TOKENS // TOK_DEV)
    expert_ids_turns = jax.random.permutation(jax.random.fold_in(own_keys[2], 3), TOKENS // TOK_DEV)
    expert_ids = jax.vmap(lambda own, number: assign_block(jax.random.fold_in(own_keys[2], 2), own, number, TOK_DEV, EXPERTS, TOPK, CAP, 1))(expert_ids_keys, expert_ids_turns).reshape((TOKENS, TOPK))
    gate_weights = jnp.clip(jnp.exp(math.log(1.0) - 2.3025851 * jax.random.uniform(own_keys[3], (TOKENS, TOPK), jnp.float32) ** steps_of(own_keys[3], (TOKENS, TOPK), ((0, 16),), -0.2, 0.2)), 0.1, 1.0)
    capacity = touch_ends(jax.random.randint(arg_keys[4], (EXPERTS,), max(1, CAP - 2), CAP + 1), jax.random.fold_in(arg_keys[4], 1), max(1, CAP - 2), CAP).astype(jnp.int32)
    expert_in = scatter_about(arg_keys[5], (EXPERTS, F, 2, D), D ** -0.5, 0.0625, ((0, 4), (1, 4)))
    expert_out = scatter_about(arg_keys[6], (EXPERTS, F, D), F ** -0.5, 0.125, ((0, 4), (1, 4)))
    return {"hidden_states": hidden_states, "norm_gain": norm_gain, "expert_ids": expert_ids, "gate_weights": gate_weights, "capacity": capacity, "expert_in": expert_in, "expert_out": expert_out}


EPSILON = 1e-06

def reference(hidden_states, norm_gain, expert_ids, gate_weights, capacity, expert_in, expert_out):
    device_count = N_EP * N_TP
    route_count = TOK_DEV * TOPK
    values = hidden_states.astype(jnp.float32)
    inverse = lax.rsqrt(lax.optimization_barrier(jnp.mean(values * values, axis=1, keepdims=True)) + EPSILON)
    normed = (values * inverse * norm_gain).astype(jnp.bfloat16)
    route_ids = expert_ids.reshape(device_count, route_count)
    onehot = (route_ids[:, :, None] == jnp.arange(EXPERTS, dtype=jnp.int32)[None, None, :]).astype(jnp.int32)
    before = lax.optimization_barrier(jnp.sum((jnp.cumsum(onehot, axis=1) - onehot) * onehot, axis=2))
    keeping = before < capacity[route_ids]
    device_index = jnp.arange(device_count, dtype=jnp.int32)[:, None]
    token_index = device_index * TOK_DEV + jnp.arange(route_count, dtype=jnp.int32)[None, :] // TOPK
    dump_slot = device_count * CAP
    position = jnp.where(keeping, device_index * CAP + before, dump_slot).astype(jnp.int32)
    table = jnp.full((EXPERTS, dump_slot + 1), TOKENS, jnp.int32)
    table = table.at[route_ids, position].set(jnp.where(keeping, token_index, TOKENS).astype(jnp.int32))
    padded = jnp.concatenate([normed, jnp.zeros((1, D), normed.dtype)], axis=0)

    def one_expert(operands):
        weight_in, weight_out, index = operands
        row_block = padded[index]
        gate_part = jnp.dot(row_block, weight_in[:, 0, :].T, preferred_element_type=jnp.float32)
        up_part = jnp.dot(row_block, weight_in[:, 1, :].T, preferred_element_type=jnp.float32)
        hidden = (jax.nn.silu(gate_part) * up_part).astype(jnp.bfloat16)
        return jnp.dot(hidden, weight_out, preferred_element_type=jnp.float32).astype(jnp.bfloat16)
    answers = lax.map(one_expert, (expert_in, expert_out, table))
    picked = answers[route_ids, position].astype(jnp.float32)
    weighting = jnp.where(keeping, gate_weights.reshape(device_count, route_count), 0.0).astype(jnp.float32)
    terms = (picked * weighting[:, :, None]).reshape(device_count, TOK_DEV, TOPK, D)
    branch_sum = lax.optimization_barrier(jnp.sum(terms, axis=2)).reshape(TOKENS, D)
    return (values + branch_sum).astype(jnp.bfloat16)
```

```python
import functools

import jax
import jax.numpy as jnp
from jax import lax
from jax.experimental import pallas as pl
from jax.experimental.pallas import tpu as pltpu
from jax.sharding import PartitionSpec as P

EPSILON = 1e-06
LANES = 128
F32 = jnp.float32
BF16 = jnp.bfloat16


def divisor(size, limit):
    fitting = [d for d in range(LANES, min(size, limit) + 1, LANES) if size % d == 0]
    return fitting[-1] if fitting else size


def partner(index, step, size):
    return index ^ step if size & (size - 1) == 0 else (index + step) % size


def prepare_kernel(hidden_ref, gain_ref, ids_ref, gates_ref, capacity_ref, out_ref):
    token_count, model_width = hidden_ref.shape
    top_count = ids_ref.shape[1]
    expert_count = capacity_ref.shape[1]
    values = hidden_ref[...].astype(F32)
    inverse = lax.rsqrt(jnp.mean(values * values, axis=1, keepdims=True) + EPSILON)
    out_ref[:, :model_width] = (values * inverse * gain_ref[...]).astype(BF16)
    lane = lax.broadcasted_iota(jnp.int32, (token_count, expert_count), 1)
    named = jnp.zeros((token_count, expert_count), F32)
    weight = jnp.zeros((token_count, expert_count), F32)
    for k in range(top_count):
        hit = ids_ref[:, k : k + 1] == lane
        named = jnp.where(hit, 1.0, named)
        weight = jnp.where(hit, gates_ref[:, k : k + 1], weight)
    row = lax.broadcasted_iota(jnp.int32, (token_count, expert_count), 0)
    before = jnp.zeros((token_count, expert_count), F32)
    for t in range(token_count - 1):
        before = before + jnp.where(row > t, named[t : t + 1, :], 0.0)
    kept = before < capacity_ref[...].astype(F32)
    weight = jnp.where(kept, weight, 0.0)
    high = weight.astype(BF16)
    rest = weight - high.astype(F32)
    middle = rest.astype(BF16)
    low = (rest - middle.astype(F32)).astype(BF16)
    pad = out_ref.shape[1] - model_width - 3 * expert_count
    terms = [high.astype(F32), middle.astype(F32), low.astype(F32), jnp.zeros((token_count, pad), F32)]
    out_ref[:, model_width:] = jnp.concatenate(terms, axis=1).astype(BF16)


def expert_kernel(
    up_steps, local_count, expert_count, first_ref, tokens_ref, in_ref, out_ref, partial_ref, weight_s, hidden_s, inner_s
):
    step = pl.program_id(1)
    unit_block, model_width = in_ref.shape[1], in_ref.shape[3]

    @pl.when(step == 0)
    def _():
        weight_s[...] = tokens_ref[:, model_width:].astype(F32).T

    @pl.when(step < up_steps)
    def _():
        hidden_s[...] = lax.dot_general(
            in_ref[0].reshape(2 * unit_block, model_width),
            tokens_ref[:, :model_width],
            (((1,), (1,)), ((), ())),
            preferred_element_type=F32,
        )
        gate = hidden_s[pl.ds(0, unit_block, stride=2), :]
        up = hidden_s[pl.ds(1, unit_block, stride=2), :]
        expert = first_ref[0] + step // (up_steps // local_count)
        weight = (
            weight_s[pl.ds(expert, 1), :]
            + weight_s[pl.ds(expert_count + expert, 1), :]
            + weight_s[pl.ds(2 * expert_count + expert, 1), :]
        )
        inner = gate / (1.0 + jnp.exp(-gate)) * up * weight
        at = pl.multiple_of(step * unit_block, unit_block)
        inner_s[:, pl.ds(at, unit_block)] = inner.T.astype(BF16)

    @pl.when(step >= up_steps)
    def _():
        partial_ref[...] = jnp.dot(inner_s[...], out_ref[...], preferred_element_type=F32).astype(BF16)


def expert_sums(tokens, weight_in, weight_out, expert_count):
    token_count, row_width = tokens.shape
    local_count, unit_count, _, model_width = weight_in.shape
    token_block = token_count if token_count <= 128 else 128
    unit_block = divisor(unit_count, 256)
    column_block = divisor(model_width, 1024)
    unit_blocks = unit_count // unit_block
    up_steps = local_count * unit_blocks
    all_units = local_count * unit_count
    first = (lax.axis_index("ep") * local_count).astype(jnp.int32).reshape(1)

    def in_map(t, p, *_):
        q = jnp.minimum(p, up_steps - 1)
        return (q // unit_blocks, q % unit_blocks, 0, 0)

    def column_of(p):
        return jnp.maximum(p - up_steps, 0)

    return pl.pallas_call(
        functools.partial(expert_kernel, up_steps, local_count, expert_count),
        out_shape=jax.ShapeDtypeStruct((token_count, model_width), BF16),
        grid_spec=pltpu.PrefetchScalarGridSpec(
            num_scalar_prefetch=1,
            grid=(token_count // token_block, up_steps + model_width // column_block),
            in_specs=[
                pl.BlockSpec((token_block, row_width), lambda t, p, *_: (t, 0)),
                pl.BlockSpec((1, unit_block, 2, model_width), in_map),
                pl.BlockSpec((all_units, column_block), lambda t, p, *_: (0, column_of(p))),
            ],
            out_specs=pl.BlockSpec((token_block, column_block), lambda t, p, *_: (t, column_of(p))),
            scratch_shapes=[
                pltpu.VMEM((row_width - model_width, token_block), F32),
                pltpu.VMEM((2 * unit_block, token_block), F32),
                pltpu.VMEM((token_block, all_units), BF16),
            ],
        ),
        compiler_params=pltpu.CompilerParams(vmem_limit_bytes=56 << 20),
        name="experts",
    )(first, tokens, weight_in, weight_out.reshape(all_units, model_width))


def shards(hidden_states, norm_gain, expert_ids, gate_weights, capacity, expert_in, expert_out):
    ep_size, tp_size = lax.axis_size("ep"), lax.axis_size("tp")
    token_count, model_width = hidden_states.shape
    expert_count = capacity.shape[0]
    tail = -(-3 * expert_count // LANES) * LANES
    own = pl.pallas_call(
        prepare_kernel,
        out_shape=jax.ShapeDtypeStruct((token_count, model_width + tail), BF16),
        name="prepare",
    )(hidden_states, norm_gain.reshape(1, -1), expert_ids, gate_weights, capacity.reshape(1, -1))

    core_size = 2 if ep_size % 2 == 0 else 1
    x_size = ep_size // core_size

    def away(core_step, x_step):
        split = [divmod(e, core_size) for e in range(ep_size)]
        return [partner(x, x_step, x_size) * core_size + partner(core, core_step, core_size) for x, core in split]

    def fetch_ep(value, core_step, x_step):
        return lax.ppermute(value, "ep", [(far, e) for e, far in enumerate(away(core_step, x_step))])

    def give_ep(value, core_step, x_step):
        return lax.ppermute(value, "ep", list(enumerate(away(core_step, x_step))))

    def fetch_tp(value, step):
        return lax.ppermute(value, "tp", [(partner(z, step, tp_size), z) for z in range(tp_size)])

    def give_tp(value, step):
        return lax.ppermute(value, "tp", [(z, partner(z, step, tp_size)) for z in range(tp_size)])

    line = [own] + [fetch_tp(own, z) for z in range(1, tp_size)]
    plane = [line] + [[fetch_ep(b, 0, x) for b in line] for x in range(1, x_size)]
    mine = jnp.concatenate([b for row in plane for b in row], axis=0)
    tokens = [mine] + [fetch_ep(mine, c, 0) for c in range(1, core_size)]
    tokens = jnp.concatenate(tokens, axis=0)

    partial_sums = expert_sums(tokens, expert_in, expert_out, expert_count)

    parts = partial_sums.reshape(core_size, x_size, tp_size, token_count, model_width)
    folded = parts[0].astype(F32)
    for c in range(1, core_size):
        folded = folded + give_ep(parts[c], c, 0).astype(F32)
    folded = folded.astype(BF16)
    total = hidden_states.astype(F32)
    for z in reversed(range(tp_size)):
        block = folded[0, z].astype(F32)
        for x in range(1, x_size):
            block = block + give_ep(folded[x, z], 0, x).astype(F32)
        if z:
            block = give_tp(block.astype(BF16), z).astype(F32)
        total = total + block
    return total.astype(BF16)


def solution(mesh):
    in_specs = (
        P(("groups", "ep", "tp"), None),
        P(),
        P(("groups", "ep", "tp"), None),
        P(("groups", "ep", "tp"), None),
        P(),
        P("ep", "tp", None, None),
        P("ep", "tp", None),
    )
    out_specs = P(("groups", "ep", "tp"), None)
    return jax.shard_map(shards, mesh=mesh, in_specs=in_specs, out_specs=out_specs, check_vma=False)
```
